32 devices in a mesh: occ: 4 (over z), vir: 8 (over y, x, core).
Axes of the slice: x: 2, y: 2, z: 4, core: 2. Of those that a mesh axis runs over, the one named last changes fastest.
Arguments:
- amplitudes: bfloat16 [352, 4096], P('occ', 'vir'), may hold values from -6 to 6
- integrals: bfloat16 [4096, 4096], P('vir', 'occ'), may hold values from -0.375 to 0.375
- labels: int32 [32], replicated, may hold values from 0 to 7
- slot_tile: int32 [32], replicated, may hold values from 0 to 31, each once
Outputs:
- residual: float32 [352, 4096], P(None, ('occ', 'vir'))
The draws below stay inside these ranges and needn't reach their ends.
Inputs may be any that keep to these rules, and one draw needn't show every extreme that they name: `slot_tile`: each tile appears in exactly one slot.
All inputs are finite; a program needn't handle non-finite values.
Results may differ from the reference program's by a relative error of at most 0.0003.
Values may be sent and summed in bfloat16 or wider, within the bound.
No kernel may reach another device: no remote copies, remote signals or barrier semaphores. Data moves between devices by JAX's collectives and lax.ppermute only.
A program may use at most 128 MiB of HBM per device.

```python
import math
import jax
import jax.numpy as jnp
import numpy as np
from jax import lax

TILE = 128
NSYM = 8
NT = 32
PAIRS = 352


def touch_ends(drawn, own_key, smallest, top_value):
    longest = drawn.shape.index(max(drawn.shape))
    spots = []
    for shift in (0, 1):
        where = [jax.random.randint(jax.random.fold_in(own_key, axis), (), 0, length) for axis, length in enumerate(drawn.shape)]
        where[longest] = (where[longest] + shift) % drawn.shape[longest]
        spots.append(tuple(where))
    return drawn.at[spots[0]].set(smallest).at[spots[1]].set(top_value)


def spiked(result, rng, source, target, shards_of, factor):
    def block_of(axis_at):
        return (jnp.arange(result.shape[axis_at]) // (result.shape[axis_at] // shards_of)).reshape((-1,) + (1,) * (result.ndim - 1 - axis_at))

    one_side = jax.random.permutation(rng, shards_of)[block_of(target)]
    far = (block_of(target) + shards_of // 2) % shards_of
    return jnp.where((block_of(source) == one_side) | (block_of(source) == far), factor * result, result)


def block_levels(stream_key, extent, split, smallest, largest):
    gain = 1.0
    for axis_at, blocks in split:
        steps = jax.random.uniform(jax.random.fold_in(jax.random.fold_in(stream_key, 6), axis_at), (blocks,), jnp.float32, smallest / len(split), largest / len(split))
        gain = gain * jnp.repeat(jnp.exp(steps), extent[axis_at] // blocks).reshape((-1,) + (1,) * (len(extent) - 1 - axis_at))
    return gain


def rank_table(number_of, lean):
    weights = [(1 << 20) // math.isqrt(grade ** lean) + 1 for grade in range(1, number_of + 1)]
    deviation = 1 + sum(weights) // (1 << 30)
    return np.cumsum(np.array([max(1, weight // deviation) for weight in weights]))


def ranked(rng, shape, count, skew):
    grid = rank_table(count, skew)
    ticket = jax.random.randint(jax.random.fold_in(rng, 1), shape, 0, int(grid[count - 1]))
    grade = jnp.searchsorted(jnp.asarray(grid, jnp.int32), ticket, side="right")
    return jax.random.permutation(jax.random.fold_in(rng, 2), count)[grade].astype(jnp.int32)


def normal_values(key, shape, scale, bound, split=(), kind=jnp.bfloat16):
    entries = scale * jax.random.normal(key, shape, jnp.float32)
    if split:
        entries = entries * block_levels(key, shape, split, -0.22, 0.18)
    return jnp.clip(entries, -bound, bound).astype(kind)


def heavy_noise(key, shape, deviation, reach, pieces, heavy, kind=jnp.bfloat16):
    array = deviation * jax.random.normal(key, shape, jnp.float32)
    if pieces:
        array = array * block_levels(key, shape, pieces, -0.22, 0.18)
    return jnp.clip(spiked(array, jax.random.fold_in(key, 3), *heavy), -reach, reach).astype(kind)


def setup_inputs(seed: int = 0) -> dict:
    seeds = jax.random.split(jax.random.key(seed), 5)
    amplitudes = normal_values(seeds[0], (PAIRS, NT * TILE), 1.0, 6.0, ((0, 4), (1, 8)))
    integrals = heavy_noise(seeds[1], (NT * TILE, NT * TILE), (NT * TILE // NSYM) ** -0.5, 0.375, ((0, 8), (1, 4)), (0, 1, 8, 2.0))
    labels = touch_ends(ranked(seeds[2], (NT,), NSYM, 2), jax.random.fold_in(seeds[2], 3), 0, NSYM - 1).astype(jnp.int32)
    slot_tile = jax.random.permutation(seeds[3], NT).astype(jnp.int32)
    return dict(amplitudes=amplitudes, integrals=integrals, labels=labels, slot_tile=slot_tile)


def reference(amplitudes, integrals, labels, slot_tile):
    slot_label = labels[slot_tile]
    row_label = jnp.repeat(slot_label, TILE)

    def one_tile(index):
        columns = lax.dynamic_slice_in_dim(integrals, index * TILE, TILE, 1)
        keep = (row_label == labels[index]).astype(jnp.bfloat16)
        masked = columns * keep[:, None]
        return jnp.dot(amplitudes, masked, preferred_element_type=jnp.float32)

    blocks = lax.map(one_tile, jnp.arange(NT, dtype=jnp.int32))
    return jnp.transpose(blocks, (1, 0, 2)).reshape(amplitudes.shape[0], NT * TILE)
```

```python
import functools

import jax
import jax.numpy as jnp
from jax import lax
from jax.experimental import pallas as pl
from jax.experimental.pallas import tpu as pltpu
from jax.sharding import PartitionSpec as P

TILE = 128
ORDER = (3, 2, 1)
CHUNKS = ((0, 3, 2), (1,))


def prepare(chips, pos_ref, labels_ref, slots_ref, x_ref, keep_ref, send_ref):
    chip, core, vir, occ = pos_ref[0], pos_ref[1], pos_ref[2], pos_ref[3]
    slots = x_ref.shape[0] // TILE
    tiles = x_ref.shape[1] // TILE
    per = tiles // (2 * chips)
    for s in range(slots):
        rows = pl.ds(s * TILE, TILE)
        have = labels_ref[slots_ref[vir * slots + s]]
        for m in range(chips):
            for q in range(per):
                for out, c in ((keep_ref, core), (send_ref, 1 - core)):
                    t = ((chip ^ m) * 2 + c) * per + q
                    match = have == labels_ref[occ * tiles + t]
                    block = x_ref[rows, pl.ds(pl.multiple_of(t * TILE, TILE), TILE)]
                    out[rows, pl.ds((m * per + q) * TILE, TILE)] = jnp.where(
                        match, block, jnp.zeros_like(block)
                    )


def shards(nocc, nvir, amplitudes, integrals, labels, slot_tile):
    chips = nvir // 2
    vir = lax.axis_index("vir")
    occ = lax.axis_index("occ")
    chip, core = vir // 2, vir % 2
    depth, cols = integrals.shape
    width = cols // nvir
    rows = amplitudes.shape[0]

    def swap(x, axis, n, m):
        return lax.ppermute(x, axis, [(i, i ^ m) for i in range(n)])

    blocks = {0: amplitudes}
    for m in ORDER:
        blocks[m] = swap(amplitudes, "occ", nocc, m)
    pos = jnp.stack([chip, core, vir, occ]).astype(jnp.int32)
    half = jax.ShapeDtypeStruct((depth, cols // 2), integrals.dtype)
    smem = pl.BlockSpec(memory_space=pltpu.SMEM)
    vmem = pl.BlockSpec(memory_space=pltpu.VMEM)
    keep, send = pl.pallas_call(
        functools.partial(prepare, chips),
        out_shape=(half, half),
        in_specs=[smem, smem, smem, vmem],
        out_specs=(vmem, vmem),
    )(pos, labels, slot_tile, integrals)
    got = swap(send, "vir", nvir, 1)

    dot = functools.partial(jnp.dot, preferred_element_type=jnp.float32)
    out = jnp.zeros((nocc * rows, width), jnp.float32)
    for chunk in CHUNKS:
        parts = []
        for z in chunk:
            mine = blocks[z]
            other = swap(mine, "vir", nvir, 1)
            parts.append(dot(mine, keep) + dot(other, got))
        part = jnp.concatenate(parts, axis=0) if len(parts) > 1 else parts[0]
        total = part[:, :width]
        for m in range(1, chips):
            piece = part[:, m * width : (m + 1) * width].astype(jnp.float16)
            total = total + swap(piece, "vir", nvir, 2 * m).astype(jnp.float32)
        for n, z in enumerate(chunk):
            out = lax.dynamic_update_slice(out, total[n * rows : (n + 1) * rows], ((occ ^ z) * rows, 0))
    return out


def solution(mesh):
    in_specs = (P("occ", "vir"), P("vir", "occ"), P(), P())
    out_specs = P(None, ("occ", "vir"))
    f = functools.partial(shards, mesh.shape["occ"], mesh.shape["vir"])
    return jax.shard_map(f, mesh=mesh, in_specs=in_specs, out_specs=out_specs, check_vma=False)
```

```python
import functools
import math

import jax
import jax.numpy as jnp
from jax import lax
from jax.experimental import pallas as pl
from jax.experimental.pallas import tpu as pltpu
from jax.sharding import PartitionSpec as P


TILE = 128
ORDER = (2, 1, 3)
CHUNKS = ((0, 2, 1), (3,))
LARGEST = 6 * 0.375
VMEM = 67_043_328
SPARE = 8 << 20


def partners(chips):
    return [(m, m + 1) for m in range(1, chips - 1, 2)], chips - 1


def layout(chips, who):
    pairs, last = partners(chips)
    owners = []
    for pair in pairs:
        owners += [(pair[who], who), (pair[who], 1 - who)]
    return owners + [(last, who), (0, who)]


def prepare(chips, labels_ref, slots_ref, x_ref, keep_ref, send_ref):
    vir, occ = lax.axis_index("vir"), lax.axis_index("occ")
    chip, core = lax.div(vir, 2), lax.rem(vir, 2)
    slots = x_ref.shape[0] // TILE
    tiles = x_ref.shape[1] // TILE
    per = tiles // (2 * chips)
    have = [labels_ref[slots_ref[vir * slots + s]] for s in range(slots)]
    for out, who in ((keep_ref, core), (send_ref, 1 - core)):
        for p, (first, second) in enumerate(zip(layout(chips, 0), layout(chips, 1))):
            offset = jnp.where(who == 0, first[0], second[0])
            owner = (chip ^ offset) * 2 + jnp.where(who == 0, first[1], second[1])
            for q in range(per):
                t = owner * per + q
                want = labels_ref[occ * tiles + t]
                for s in range(slots):
                    rows = pl.ds(s * TILE, TILE)
                    block = x_ref[rows, pl.ds(pl.multiple_of(t * TILE, TILE), TILE)]
                    out[rows, pl.ds((p * per + q) * TILE, TILE)] = jnp.where(
                        have[s] == want, block, jnp.zeros_like(block)
                    )


def multiply(n, widths, start, *refs):
    mine, other, (keep_ref, got_ref) = refs[:n], refs[n : 2 * n], refs[2 * n : 2 * n + 2]
    outs, (left, right) = refs[2 * n + 2 : -2], refs[-2:]
    rows = mine[0].shape[0]
    for at in range(n):
        left[pl.ds(at * rows, rows), :] = mine[at][...]
        right[pl.ds(at * rows, rows), :] = other[at][...]
    for out, width in zip(outs, widths):
        cols = pl.ds(start, width)
        out[...] = jnp.dot(
            left[...], keep_ref[:, cols], preferred_element_type=jnp.float32
        ) + jnp.dot(right[...], got_ref[:, cols], preferred_element_type=jnp.float32)
        start += width


def contract(order, chunks, nocc, nvir, amplitudes, integrals, labels, slot_tile):
    chips = nvir // 2
    pairs, last = partners(chips)
    depth, cols = integrals.shape
    rows = amplitudes.shape[0]
    width = cols // nvir
    scale = 2.0 ** math.floor(math.log2(65504 / (2 * depth * LARGEST)))

    def swap(x, axis, to):
        n = {"occ": nocc, "vir": nvir}[axis]
        return lax.ppermute(x, axis, [(i, to(i)) for i in range(n)])

    blocks = {0: amplitudes}
    for m in order:
        blocks[m] = swap(amplitudes, "occ", lambda i: i ^ m)
    near = functools.partial(pltpu.with_memory_space_constraint, memory_space=pltpu.VMEM)
    half = pltpu.VMEM((depth, cols // 2), integrals.dtype)
    smem = pl.BlockSpec(memory_space=pltpu.SMEM)
    vmem = pl.BlockSpec(memory_space=pltpu.VMEM)
    keep, send = pl.pallas_call(
        functools.partial(prepare, chips),
        out_shape=(half, half),
        in_specs=[smem, smem, vmem],
        out_specs=(vmem, vmem),
        compiler_params=pltpu.CompilerParams(vmem_limit_bytes=VMEM - 7 * integrals.size),
    )(labels, slot_tile, integrals)
    got = swap(send, "vir", lambda i: i ^ 1)

    def products(chunk, start, *widths):
        n = len(chunk)
        mine = [near(blocks[m]) for m in chunk]
        return pl.pallas_call(
            functools.partial(multiply, n, widths, start),
            out_shape=tuple(pltpu.VMEM((n * rows, w), jnp.float32) for w in widths),
            in_specs=[vmem] * (2 * n + 2),
            out_specs=(vmem,) * len(widths),
            scratch_shapes=[pltpu.VMEM((n * rows, depth), amplitudes.dtype)] * 2,
            compiler_params=pltpu.CompilerParams(vmem_limit_bytes=4 * n * rows * depth + SPARE),
        )(*mine, *(others[m] for m in chunk), near(keep), near(got))

    def narrow(x):
        return (x * scale).astype(jnp.float16)

    others, sums = {}, []
    for chunk in chunks:
        for m in chunk:
            others[m] = near(swap(blocks[m], "vir", lambda i: i ^ 1))
        *wide, far = products(chunk, 0, *[2 * width] * len(pairs), width)
        kept, passed = [], []
        for pair, part in zip(pairs, wide):
            part = swap(narrow(part), "vir", lambda v: v ^ (2 * pair[v % 2]))
            kept.append(part[:, :width])
            passed.append(swap(part[:, width:], "vir", lambda v: v ^ 1))
        kept.append(swap(narrow(far), "vir", lambda v: v ^ (2 * last)))
        (local,) = products(chunk, (chips - 1) * width, width)
        sums.append(local + sum(x.astype(jnp.float32) for x in kept + passed) * (1 / scale))
    occ = lax.axis_index("occ")
    out = jnp.zeros((nocc * rows, width), jnp.float32)
    for chunk, total in zip(chunks, sums):
        for n, m in enumerate(chunk):
            out = lax.dynamic_update_slice(out, total[n * rows : (n + 1) * rows], ((occ ^ m) * rows, 0))
    return out


def solution(mesh):

    def shards(*args):
        return contract(ORDER, CHUNKS, mesh.shape["occ"], mesh.shape["vir"], *args)

    in_specs = (P("occ", "vir"), P("vir", "occ"), P(), P())
    out_specs = P(None, ("occ", "vir"))
    return jax.shard_map(shards, mesh=mesh, in_specs=in_specs, out_specs=out_specs, check_vma=False)
```
